32 devices in a mesh: blk: 4 (over x, core), shard: 8 (over z, y).
Axes of the slice: x: 2, y: 2, z: 4, core: 2. Of those that a mesh axis runs over, the one named last changes fastest.
Arguments:
- item_features: bfloat16 [32768, 1024], P('shard'), may hold values from -6 to 6
- tower_weight: bfloat16 [1024, 512], replicated, may hold values from -0.1875 to 0.1875
- gate_in: bfloat16 [64, 128], replicated, may hold values from -0.75 to 0.75
- gate_in_bias: bfloat16 [128], replicated, may hold values from -4 to 4
- gate_out: bfloat16 [128, 64], replicated, may hold values from -0.5 to 0.5
- gate_out_bias: bfloat16 [64], replicated, may hold values from -4 to 4
- user_table: bfloat16 [4096, 512], P(('blk', 'shard')), may hold values from -6 to 6
- user_ids: int32 [128], P(('blk', 'shard')), may hold values from 0 to 127
- positive_item: int32 [128, 16], P(('blk', 'shard')), may hold values from 0 to 2047
- listed_owner: int32 [128, 1], P(('blk', 'shard')), may hold values from 0 to 7; in each aligned block of 4 rows (0 to 3, 4 to 7, ...) at most 2 rows name the same one
- listed_slot: int32 [128], P(('blk', 'shard')), may hold values from 0 to 31
Outputs:
- tower_gradient: float32 [1024, 512], P('shard')
- user_gradient: float32 [4096, 512], P(('blk', 'shard'))
The draws below stay inside these ranges and needn't reach their ends.
Inputs may be any that keep to these rules, and one draw needn't show every extreme that they name: `listed_owner`: at most 2 of the 4 listings of one trainer name the same owner. `user_ids`: A row of the trainer's own 128 rows of user_table. `positive_item`: A position among the rows of the user's circle.
All inputs are finite; a program needn't handle non-finite values.
Results may differ from the reference program's by a relative error of at most 0.0055.
Values may be sent and summed in bfloat16 or wider, within the bound.
A program may use at most 128 MiB of HBM per device.

```python
import math
import jax
import jax.numpy as jnp
import numpy as np
from jax import lax

F = 1024
K = 8
H = 64
G = 128
BLK = 128
CAP = 2
POS = 16
OWN = 32
USERS = 4
UTAB = 128
LIST = 4
E = 512
P_SIZE = 64
GROUPS = 4
OWNERS = 8
TRAINERS = 32
CIRCLE = 2048


def plant(entries, stream_key, low, high):
    longest = entries.shape.index(max(entries.shape))
    spots = []
    for shift in (0, 1):
        where = [jax.random.randint(jax.random.fold_in(stream_key, axis), (), 0, length) for axis, length in enumerate(entries.shape)]
        where[longest] = (where[longest] + shift) % entries.shape[longest]
        spots.append(tuple(where))
    return entries.at[spots[0]].set(low).at[spots[1]].set(high)


def with_spikes(array, key, source, target, parts, factor):
    def block_of(axis_at):
        return (jnp.arange(array.shape[axis_at]) // (array.shape[axis_at] // parts)).reshape((-1,) + (1,) * (array.ndim - 1 - axis_at))

    near = jax.random.permutation(key, parts)[block_of(target)]
    far = (block_of(target) + parts // 2) % parts
    return jnp.where((block_of(source) == near) | (block_of(source) == far), factor * array, array)


def block_scale(stream_key, dims, cuts, low, high):
    loudness = 1.0
    for axis_at, parts in cuts:
        steps = jax.random.uniform(jax.random.fold_in(jax.random.fold_in(stream_key, 6), axis_at), (parts,), jnp.float32, low / len(cuts), high / len(cuts))
        loudness = loudness * jnp.repeat(jnp.exp(steps), dims[axis_at] // parts).reshape((-1,) + (1,) * (len(dims) - 1 - axis_at))
    return loudness


def assign_block(key, own, number, rows, amount, top, reach, slope):
    ranking = jax.random.permutation(key, amount)
    crowded, ordinary = shares(amount, rows * top, reach, slope, True), shares(amount, rows * top, reach, slope, False)
    places = jnp.arange(amount)

    def named(tallies, rotation):
        used = int((tallies > 0).sum())
        fixed = max(1, used // 4)
        shifted = fixed + (places - fixed + rotation * (used - fixed)) % max(1, amount - fixed)
        return jnp.zeros((amount,), jnp.int32).at[ranking[jnp.where(places < fixed, places, shifted)]].set(jnp.asarray(tallies, jnp.int32))

    tallies = jnp.where(number % 4 == 0, named(crowded, number // 4), named(ordinary, number - number // 4 - 1))
    mixed = jax.random.permutation(jax.random.fold_in(own, 3), amount)
    donor, sink = mixed[0:amount // 2 * 2:2], mixed[1:amount // 2 * 2:2]
    margin = jnp.minimum(tallies[donor] - 1, reach - tallies[sink]) // 2
    margin = jnp.where((donor == ranking[0]) | (sink == ranking[0]) | (tallies[sink] == 0), 0, jnp.maximum(margin, 0))
    shifted = jax.random.randint(jax.random.fold_in(own, 4), (amount // 2,), 0, 1 << 20) % (margin + 1)
    tallies = tallies.at[donor].add(-shifted).at[sink].add(shifted)
    labels = jnp.searchsorted(jnp.cumsum(tallies), jnp.arange(rows * top), side="right").astype(jnp.int32)
    grid = labels.reshape(top, rows).T
    grid = grid[jax.random.permutation(jax.random.fold_in(own, 1), rows)]
    rotation = jax.random.randint(jax.random.fold_in(own, 2), (rows, 1), 0, top)
    return jnp.take_along_axis(grid, (jnp.arange(top)[None, :] + rotation) % top, axis=1)


def shares(count, total, most, skew, full):
    portions = [(1 << 20) // math.isqrt(grade ** skew) + 1 for grade in range(1, count + 1)]
    largest = most if full else min(most, max(-(-total // count), total * portions[0] // sum(portions)))
    least = 1 if total - largest >= count - 1 else 0
    holding, surplus = [largest] + [least] * (count - 1), total - largest - least * (count - 1)
    while surplus > 0:
        candidates = [i for i in range(1, count) if holding[i] < largest] or [i for i in range(1, count) if holding[i] < most]
        pool, left = sum([portions[i] for i in candidates]), surplus
        for i in candidates:
            extra = min(most - holding[i], max(1, left * portions[i] // pool), surplus)
            holding[i] = holding[i] + extra
            surplus = surplus - extra
    return np.array(holding)


def noise(rng, shape, deviation, limit, split=(), kind=jnp.bfloat16):
    values = deviation * jax.random.normal(rng, shape, jnp.float32)
    if split:
        values = values * block_scale(rng, shape, split, -0.22, 0.18)
    return jnp.clip(values, -limit, limit).astype(kind)


def noise_with(rng, extent, width, limit, pieces, heavy, kind=jnp.bfloat16):
    entries = width * jax.random.normal(rng, extent, jnp.float32)
    if pieces:
        entries = entries * block_scale(rng, extent, pieces, -0.22, 0.18)
    return jnp.clip(with_spikes(entries, jax.random.fold_in(rng, 3), *heavy), -limit, limit).astype(kind)


def setup_inputs(seed: int = 0) -> dict:
    key_of = jax.random.split(jax.random.key(seed), 12)
    item_features = noise_with(key_of[0], (OWNERS * OWN * BLK, F), 1.0, 6.0, ((0, 8),), (0, 1, 8, 2.0))
    tower_weight = noise(key_of[1], (F, E), F ** -0.5, 0.1875)
    gate_in = noise(key_of[2], (P_SIZE, G), P_SIZE ** -0.5, 0.75)
    gate_in_bias = noise(key_of[3], (G,), 1.0, 4.0)
    gate_out = noise(key_of[4], (G, P_SIZE), G ** -0.5, 0.5)
    gate_out_bias = noise(key_of[5], (P_SIZE,), 1.0, 4.0)
    user_table = noise(key_of[6], (TRAINERS * UTAB, E), 1.0, 6.0, ((0, 32),))
    user_ids = plant(jax.random.randint(key_of[7], (TRAINERS * USERS,), 0, UTAB), jax.random.fold_in(key_of[7], 1), 0, UTAB - 1).astype(jnp.int32)
    positive_item = plant(jax.random.randint(key_of[8], (TRAINERS * USERS, POS), 0, CIRCLE), jax.random.fold_in(key_of[8], 1), 0, CIRCLE - 1).astype(jnp.int32)
    listed_owner_keys = jax.random.split(jax.random.fold_in(key_of[9], 1), (TRAINERS * LIST) // LIST)
    listed_owner_turns = jax.random.permutation(jax.random.fold_in(key_of[9], 3), (TRAINERS * LIST) // LIST)
    listed_owner = jax.vmap(lambda own, number: assign_block(jax.random.fold_in(key_of[9], 2), own, number, LIST, OWNERS, 1, CAP, 2))(listed_owner_keys, listed_owner_turns).reshape((TRAINERS * LIST, 1))
    listed_slot = plant(jax.random.randint(key_of[10], (TRAINERS * LIST,), 0, OWN), jax.random.fold_in(key_of[10], 1), 0, OWN - 1).astype(jnp.int32)
    return dict(item_features=item_features, tower_weight=tower_weight, gate_in=gate_in, gate_in_bias=gate_in_bias, gate_out=gate_out, gate_out_bias=gate_out_bias, user_table=user_table, user_ids=user_ids, positive_item=positive_item, listed_owner=listed_owner, listed_slot=listed_slot)


def pair_terms(user_rows, item_rows, targets, gate_in, gate_in_bias, gate_out, gate_out_bias):
    count_users = user_rows.shape[0]
    count_items = item_rows.shape[0]
    scaling = 1.0 / math.sqrt(H)
    user_parts = user_rows.astype(jnp.float32).reshape(count_users * K, H)
    item_parts = item_rows.astype(jnp.float32).reshape(count_items, K, H)
    logits = jnp.einsum('xh,ibh->xbi', user_parts, item_parts) * scaling
    logits = logits.reshape(count_users, K * K, count_items)
    gate_input = logits.astype(jnp.bfloat16)
    first_layer = gate_in.astype(jnp.float32)
    second_layer = gate_out.astype(jnp.float32)
    hidden_pre = jnp.einsum('pg,upi->ugi', first_layer, gate_input.astype(jnp.float32))
    hidden_pre = hidden_pre + gate_in_bias.astype(jnp.float32)[None, :, None]
    hidden = jax.nn.silu(hidden_pre).astype(jnp.bfloat16)
    gate_logit = jnp.einsum('gp,ugi->upi', second_layer, hidden.astype(jnp.float32))
    gate_logit = gate_logit + gate_out_bias.astype(jnp.float32)[None, :, None]
    exp_terms = jnp.exp(gate_logit)
    mixture = exp_terms / lax.optimization_barrier(jnp.sum(exp_terms, axis=1, keepdims=True))
    scores = lax.optimization_barrier(jnp.sum(mixture * logits, axis=1))
    score_grad = jax.nn.sigmoid(scores) - targets
    weighted = score_grad[:, None, :] * mixture
    logit_grad = (weighted * (logits - scores[:, None, :])).astype(jnp.bfloat16)
    gate_sig = jax.nn.sigmoid(hidden_pre)
    hidden_grad = jnp.einsum('gp,upi->ugi', second_layer, logit_grad.astype(jnp.float32))
    hidden_grad = (hidden_grad * gate_sig * (1.0 + hidden_pre * (1.0 - gate_sig))).astype(jnp.bfloat16)
    pair_grad = weighted + jnp.einsum('pg,ugi->upi', first_layer, hidden_grad.astype(jnp.float32))
    pair_grad = pair_grad.astype(jnp.bfloat16).astype(jnp.float32).reshape(count_users * K, K, count_items)
    user_delta = jnp.einsum('xbi,ibh->xh', pair_grad, item_parts).reshape(count_users, K * H) * scaling
    item_delta = jnp.einsum('xbi,xh->ibh', pair_grad, user_parts).reshape(count_items, K * H) * scaling
    return (user_delta, item_delta)

def reference(item_features, tower_weight, gate_in, gate_in_bias, gate_out, gate_out_bias, user_table, user_ids, positive_item, listed_owner, listed_slot):
    vectors = jnp.dot(item_features, tower_weight, preferred_element_type=jnp.float32).astype(jnp.bfloat16)
    vectors = vectors.reshape(OWNERS * OWN, BLK, E)
    block_ids = (listed_owner[:, 0] * OWN + listed_slot).astype(jnp.int32)
    listed = jnp.take(vectors, block_ids, axis=0).reshape(GROUPS, OWNERS, LIST * BLK, E)
    tables = user_table.reshape(TRAINERS, UTAB, E)
    row_ids = user_ids.reshape(TRAINERS, USERS).astype(jnp.int32)
    user_rows = jnp.take_along_axis(tables, row_ids[:, :, None], axis=1).reshape(GROUPS, OWNERS, USERS, E)
    targets = positive_item.reshape(GROUPS, OWNERS, USERS, POS)
    columns = jnp.arange(CIRCLE, dtype=jnp.int32)

    def column(column_index):
        col_users = lax.dynamic_index_in_dim(user_rows, column_index, 1, keepdims=False).reshape(GROUPS * USERS, E)
        col_items = lax.dynamic_index_in_dim(listed, column_index, 1, keepdims=False).reshape(CIRCLE, E)
        col_pos = lax.dynamic_index_in_dim(targets, column_index, 1, keepdims=False).reshape(GROUPS * USERS, POS)
        matches = jnp.any(col_pos[:, :, None] == columns[None, None, :], axis=1).astype(jnp.float32)
        return pair_terms(col_users, col_items, matches, gate_in, gate_in_bias, gate_out, gate_out_bias)
    user_delta, item_delta = lax.map(column, jnp.arange(OWNERS, dtype=jnp.int32))
    listing_grads = item_delta.astype(jnp.bfloat16).reshape(OWNERS, GROUPS, LIST, BLK, E)
    listing_grads = jnp.transpose(listing_grads, (1, 0, 2, 3, 4)).reshape(TRAINERS * LIST, BLK, E)
    per_block = jax.ops.segment_sum(listing_grads.astype(jnp.float32), block_ids, num_segments=OWNERS * OWN)
    per_block = per_block.reshape(OWNERS * OWN * BLK, E)
    tower_gradient = lax.dot_general(item_features.astype(jnp.float32), per_block, (((0,), (0,)), ((), ())), precision=lax.Precision.HIGHEST)
    user_deltas = jnp.transpose(user_delta.reshape(OWNERS, GROUPS, USERS, E), (1, 0, 2, 3)).reshape(TRAINERS, USERS, E)
    row_hot = (row_ids[:, :, None] == jnp.arange(UTAB, dtype=jnp.int32)[None, None, :]).astype(jnp.float32)
    user_gradient = jnp.einsum('tkr,tke->tre', row_hot, user_deltas, precision=lax.Precision.HIGHEST)
    return (tower_gradient, user_gradient.reshape(TRAINERS * UTAB, E))
```

```python
import functools
import math

import jax
import jax.numpy as jnp
from jax import lax
from jax.experimental import pallas as pl
from jax.experimental.pallas import tpu as pltpu
from jax.sharding import PartitionSpec as P

K = 8
H = 64
BLK = 128
CAP = 2
LANES = 128
CHUNK = 4

NN = (((1,), (0,)), ((), ()))
NT = (((1,), (1,)), ((), ()))


def dot(left, right, dims=NN):
    return lax.dot_general(left, right, dims, preferred_element_type=jnp.float32)


def sigmoid(v):
    return 0.5 + 0.5 * jnp.tanh(0.5 * v)


def pair_kernel(
    groups,
    owners,
    users,
    count_ref,
    block_ref,
    column_ref,
    base_ref,
    feat_ref,
    tower_ref,
    users_ref,
    users_t_ref,
    pos_ref,
    gin_ref,
    gin_t_ref,
    gin_b_ref,
    gout_ref,
    gout_t_ref,
    gout_b_ref,
    out_ref,
    acc,
    uacc,
    logit_s,
    pair_s,
):
    step = pl.program_id(0)
    column_users = groups * users
    rows = column_users * K

    @pl.when(step == 0)
    def _():
        acc[...] = jnp.zeros_like(acc)
        uacc[...] = jnp.zeros_like(uacc)

    @pl.when(step < count_ref[0])
    def _():
        column = column_ref[step]
        base = base_ref[step]
        feat = feat_ref[...]
        vec_t = dot(tower_ref[...], feat, NT).astype(jnp.bfloat16)
        vec_cat = jnp.concatenate([vec_t[b * H : (b + 1) * H] for b in range(K)], axis=1)
        logit_s[...] = dot(users_ref[column], vec_cat)
        pos = pos_ref[column]
        place = base + lax.broadcasted_iota(jnp.int32, (column_users, BLK), 1)
        hit = pos[:, 0:1] == place
        for k in range(1, pos.shape[1]):
            hit = jnp.logical_or(hit, pos[:, k : k + 1] == place)
        target = jnp.where(hit, 1.0, 0.0)
        for first in range(0, column_users, CHUNK):
            picked = range(first, first + CHUNK)
            logits = jnp.concatenate(
                [
                    jnp.concatenate(
                        [
                            logit_s[u * K : (u + 1) * K, b * BLK : (b + 1) * BLK]
                            for b in range(K)
                        ],
                        axis=0,
                    )
                    for u in picked
                ],
                axis=1,
            )
            wanted = jnp.concatenate([target[u : u + 1] for u in picked], axis=1)
            pre = dot(gin_t_ref[...], logits.astype(jnp.bfloat16)) + gin_b_ref[...]
            sig = sigmoid(pre)
            silu = pre * sig
            slope = sig + silu * (1.0 - sig)
            gate = dot(gout_t_ref[...], silu.astype(jnp.bfloat16)) + gout_b_ref[...]
            terms = jnp.exp(gate)
            mixture = terms * (1.0 / jnp.sum(terms, axis=0, keepdims=True))
            scores = jnp.sum(mixture * logits, axis=0, keepdims=True)
            score_grad = sigmoid(scores) - wanted
            weighted = score_grad * mixture
            logit_grad = (weighted * (logits - scores)).astype(jnp.bfloat16)
            hidden_grad = (dot(gout_ref[...], logit_grad) * slope).astype(jnp.bfloat16)
            pair = weighted + dot(gin_ref[...], hidden_grad)
            for n, u in enumerate(picked):
                for b in range(K):
                    pair_s[u * K : (u + 1) * K, b * BLK : (b + 1) * BLK] = pair[
                        b * K : (b + 1) * K, n * BLK : (n + 1) * BLK
                    ]
        pair_all = pair_s[...].astype(jnp.bfloat16)
        uacc[column] += dot(pair_all, vec_cat, NT)
        grad = dot(users_t_ref[column], pair_all).astype(jnp.bfloat16)
        grad_t = jnp.concatenate([grad[:, b * BLK : (b + 1) * BLK] for b in range(K)], axis=0)
        acc[...] += dot(grad_t, feat)

    @pl.when(step == pl.num_programs(0) - 1)
    def _():
        width = acc.shape[1] // owners
        height = acc.shape[0] // groups
        share = rows // groups
        out_ref[...] = jnp.zeros_like(out_ref)
        for g in range(groups):
            for s in range(owners):
                out_ref[g, s, 0:height, 0:width] = acc[
                    g * height : (g + 1) * height, s * width : (s + 1) * width
                ].astype(jnp.bfloat16)
                out_ref[g, s, height : height + share, 0:H] = (
                    uacc[s, g * share : (g + 1) * share] * (1.0 / math.sqrt(H))
                ).astype(jnp.bfloat16)


def sum_kernel(
    groups,
    owners,
    in_ref,
    tower_out,
    user_out,
    recv1,
    stage,
    recv2,
    part,
    final,
    send1,
    rsem1,
    send2,
    rsem2,
    send3,
    rsem3,
):
    g = lax.axis_index("blk")
    s = lax.axis_index("shard")
    height = part.shape[0]
    width = tower_out.shape[0]

    barrier = pltpu.get_barrier_semaphore()
    for d in range(1, groups):
        pl.semaphore_signal(
            barrier, inc=1, device_id=(lax.rem(g + d, groups), s),
            device_id_type=pl.DeviceIdType.MESH,
        )
    for d in range(1, owners):
        pl.semaphore_signal(
            barrier, inc=1, device_id=(g, lax.rem(s + d, owners)),
            device_id_type=pl.DeviceIdType.MESH,
        )
    pl.semaphore_wait(barrier, groups + owners - 2)

    copies = []
    for d in range(1, groups):
        to = lax.rem(g + d, groups)
        copy = pltpu.make_async_remote_copy(
            src_ref=in_ref.at[to], dst_ref=recv1.at[d - 1],
            send_sem=send1.at[d - 1], recv_sem=rsem1.at[d - 1],
            device_id=(to, s), device_id_type=pl.DeviceIdType.MESH,
        )
        copy.start()
        copies.append(copy)
    for copy in copies:
        copy.wait()
    total = in_ref[g].astype(jnp.float32)
    for d in range(1, groups):
        total = total + recv1[d - 1].astype(jnp.float32)
    stage[...] = total.astype(jnp.bfloat16)

    copies = []
    for d in range(1, owners):
        to = lax.rem(s + d, owners)
        copy = pltpu.make_async_remote_copy(
            src_ref=stage.at[to], dst_ref=recv2.at[d - 1],
            send_sem=send2.at[d - 1], recv_sem=rsem2.at[d - 1],
            device_id=(g, to), device_id_type=pl.DeviceIdType.MESH,
        )
        copy.start()
        copies.append(copy)
    for copy in copies:
        copy.wait()
    mine = stage[s].astype(jnp.float32)
    for d in range(1, owners):
        mine = mine + recv2[d - 1].astype(jnp.float32)
    user_out[...] = mine[height:, :]
    part[...] = mine[:height, :]

    copies = []
    for d in range(1, groups):
        to = lax.rem(g + d, groups)
        copy = pltpu.make_async_remote_copy(
            src_ref=part, dst_ref=final.at[g],
            send_sem=send3.at[d - 1], recv_sem=rsem3.at[d - 1],
            device_id=(to, s), device_id_type=pl.DeviceIdType.MESH,
        )
        copy.start()
        copies.append(copy)
    final[g] = part[...]
    for copy in copies:
        copy.wait()
    for r in range(groups):
        tower_out[:, r * height : (r + 1) * height] = final[r].T[:width]


def swap(weights):
    return weights.reshape((K, K) + weights.shape[1:]).swapaxes(0, 1).reshape(weights.shape)


def shards(
    item_features,
    tower_weight,
    gate_in,
    gate_in_bias,
    gate_out,
    gate_out_bias,
    user_table,
    user_ids,
    positive_item,
    listed_owner,
    listed_slot,
):
    groups = lax.axis_size("blk")
    owners = lax.axis_size("shard")
    g = lax.axis_index("blk")
    s = lax.axis_index("shard")
    trainers = groups * owners
    listings = listed_slot.shape[0]
    users, picks = positive_item.shape
    table = user_table.shape[0]
    features = item_features.shape[1]
    embed = tower_weight.shape[1]
    hidden = gate_in.shape[1]
    column_users = groups * users
    rows = column_users * K
    circle_part = listings * BLK

    row_match = user_ids[:, None] == jnp.arange(table, dtype=jnp.int32)[None, :]
    user_rows = jnp.dot(
        row_match.astype(jnp.bfloat16), user_table, preferred_element_type=jnp.float32
    ).astype(jnp.bfloat16)
    flat_pos = positive_item.reshape(-1)
    numbers = jnp.concatenate([flat_pos // 128, flat_pos % 128, listed_owner[:, 0], listed_slot])
    number_row = jnp.zeros((1, embed), jnp.bfloat16).at[0, : numbers.shape[0]].set(
        numbers.astype(jnp.bfloat16)
    )
    packet = jnp.concatenate([user_rows, number_row], axis=0)
    packet = jnp.pad(packet, ((0, 16 - users - 1), (0, 0)))
    gathered = lax.all_gather(packet, ("blk", "shard"), axis=0, tiled=False)
    all_users = gathered[:, :users].reshape(groups, owners, users * K, H)
    all_users = all_users.swapaxes(0, 1).reshape(owners, rows, H)
    all_users = (all_users.astype(jnp.float32) * (1.0 / math.sqrt(H))).astype(jnp.bfloat16)
    all_users_t = all_users.swapaxes(1, 2)
    back = gathered[:, users].astype(jnp.float32).astype(jnp.int32)
    span = users * picks
    all_pos = (back[:, :span] * 128 + back[:, span : 2 * span]).reshape(
        groups, owners, users, picks
    )
    all_pos = all_pos.swapaxes(0, 1).reshape(owners, column_users, picks)
    all_owner = back[:, 2 * span : 2 * span + listings].reshape(-1)
    all_slot = back[:, 2 * span + listings : 2 * span + 2 * listings].reshape(-1)

    entries = trainers * listings
    most = -(-trainers * min(CAP, listings) // groups)
    entry = jnp.arange(entries, dtype=jnp.int32)
    own = all_owner == s
    rank = jnp.sum(
        jnp.where(jnp.logical_and(own[None, :], entry[None, :] < entry[:, None]), 1, 0), axis=1
    )
    count = (jnp.sum(own.astype(jnp.int32)) - g + groups - 1) // groups
    place = jnp.minimum(jnp.arange(most, dtype=jnp.int32), jnp.maximum(count - 1, 0))
    chosen = jnp.logical_and(own[None, :], rank[None, :] == place[:, None] * groups + g)

    def choose(values):
        return jnp.sum(jnp.where(chosen, values[None, :], 0), axis=1)

    trainer = entry // listings
    unit_block = choose(all_slot)
    unit_column = choose(trainer % owners)
    unit_base = choose((trainer // owners) * circle_part + (entry % listings) * BLK)

    gin = swap(gate_in)
    gout_t = swap(gate_out.T)
    height = embed // groups
    width = features // owners
    out_rows = height + users * K

    def whole(shape):
        return pl.BlockSpec(shape, lambda i, *_: (0,) * len(shape))

    terms = pl.pallas_call(
        functools.partial(pair_kernel, groups, owners, users),
        grid_spec=pltpu.PrefetchScalarGridSpec(
            num_scalar_prefetch=4,
            grid=(most,),
            in_specs=[
                pl.BlockSpec((BLK, features), lambda i, c, b, *_: (b[i], 0)),
                whole((embed, features)),
                whole((owners, rows, H)),
                whole((owners, H, rows)),
                whole((owners, column_users, picks)),
                whole((K * K, hidden)),
                whole((hidden, K * K)),
                whole((hidden, 1)),
                whole((hidden, K * K)),
                whole((K * K, hidden)),
                whole((K * K, 1)),
            ],
            out_specs=whole((groups, owners, out_rows, LANES)),
            scratch_shapes=[
                pltpu.VMEM((embed, features), jnp.float32),
                pltpu.VMEM((owners, rows, H), jnp.float32),
                pltpu.VMEM((rows, K * BLK), jnp.float32),
                pltpu.VMEM((rows, K * BLK), jnp.float32),
            ],
        ),
        out_shape=jax.ShapeDtypeStruct((groups, owners, out_rows, LANES), jnp.bfloat16),
        compiler_params=pltpu.CompilerParams(
            dimension_semantics=("arbitrary",), vmem_limit_bytes=56 << 20
        ),
    )(
        count.reshape(1),
        unit_block,
        unit_column,
        unit_base,
        item_features,
        tower_weight.T,
        all_users,
        all_users_t,
        all_pos,
        gin,
        gin.T,
        gate_in_bias.astype(jnp.float32)[:, None],
        gout_t.T,
        gout_t,
        swap(gate_out_bias.astype(jnp.float32))[:, None],
    )

    tower_gradient, user_terms = pl.pallas_call(
        functools.partial(sum_kernel, groups, owners),
        out_shape=(
            jax.ShapeDtypeStruct((width, embed), jnp.float32),
            jax.ShapeDtypeStruct((users * K, LANES), jnp.float32),
        ),
        in_specs=[pl.BlockSpec(memory_space=pltpu.VMEM)],
        out_specs=(
            pl.BlockSpec(memory_space=pltpu.VMEM),
            pl.BlockSpec(memory_space=pltpu.VMEM),
        ),
        scratch_shapes=[
            pltpu.VMEM((groups - 1, owners, out_rows, LANES), jnp.bfloat16),
            pltpu.VMEM((owners, out_rows, LANES), jnp.bfloat16),
            pltpu.VMEM((owners - 1, out_rows, LANES), jnp.bfloat16),
            pltpu.VMEM((height, LANES), jnp.float32),
            pltpu.VMEM((groups, height, LANES), jnp.float32),
            pltpu.SemaphoreType.DMA((groups - 1,)),
            pltpu.SemaphoreType.DMA((groups - 1,)),
            pltpu.SemaphoreType.DMA((owners - 1,)),
            pltpu.SemaphoreType.DMA((owners - 1,)),
            pltpu.SemaphoreType.DMA((groups - 1,)),
            pltpu.SemaphoreType.DMA((groups - 1,)),
        ],
        compiler_params=pltpu.CompilerParams(collective_id=0, has_side_effects=True),
    )(terms)

    user_delta = user_terms[:, :H].reshape(users, embed)
    user_gradient = jnp.sum(
        jnp.where(row_match[:, :, None], user_delta[:, None, :], 0.0), axis=0
    )
    return (tower_gradient, user_gradient)


def solution(mesh):
    return jax.shard_map(
        shards,
        mesh=mesh,
        in_specs=(
            P("shard", None),
            P(),
            P(),
            P(),
            P(),
            P(),
            P(("blk", "shard"), None),
            P(("blk", "shard")),
            P(("blk", "shard"), None),
            P(("blk", "shard"), None),
            P(("blk", "shard")),
        ),
        out_specs=(P("shard", None), P(("blk", "shard"), None)),
        check_vma=False,
    )
```

```python
import functools
import math

import jax
import jax.numpy as jnp
from jax import lax
from jax.experimental import pallas as pl
from jax.experimental.pallas import tpu as pltpu
from jax.sharding import PartitionSpec as P

K = 8
H = 64
BLK = 128
CAP = 2
LANES = 128
CHUNK = 4

NN = (((1,), (0,)), ((), ()))
NT = (((1,), (1,)), ((), ()))


def dot(left, right, dims=NN):
    return lax.dot_general(left, right, dims, preferred_element_type=jnp.float32)


def sigmoid(v):
    return 0.5 + 0.5 * jnp.tanh(0.5 * v)


def pair_kernel(
    groups,
    owners,
    users,
    count_ref,
    block_ref,
    column_ref,
    base_ref,
    feat_ref,
    tower_ref,
    packet_ref,
    gin_in,
    gin_b_in,
    gout_in,
    gout_b_in,
    out_ref,
    acc,
    uacc,
    logit_s,
    pair_s,
    gin_ref,
    gin_t_ref,
    gin_b_ref,
    gout_ref,
    gout_t_ref,
    gout_b_ref,
    *,
    picks,
):
    step = pl.program_id(0)
    column_users = groups * users
    rows = column_users * K

    @pl.when(step == 0)
    def _():
        acc[...] = jnp.zeros_like(acc)
        uacc[...] = jnp.zeros_like(uacc)
        pairs = K * K
        to = lax.broadcasted_iota(jnp.int32, (pairs, pairs), 0)
        of = lax.broadcasted_iota(jnp.int32, (pairs, pairs), 1)
        turn = jnp.where(of == (to % K) * K + to // K, 1.0, 0.0).astype(jnp.bfloat16)
        gin = dot(turn, gin_in[...])
        gin_ref[...] = gin.astype(jnp.bfloat16)
        gin_t_ref[...] = gin.T.astype(jnp.bfloat16)
        gout = dot(gout_in[...], turn, NT)
        gout_ref[...] = gout.astype(jnp.bfloat16)
        gout_t_ref[...] = gout.T.astype(jnp.bfloat16)

        def stand(row):
            return jnp.broadcast_to(row.astype(jnp.float32), (LANES, row.shape[1])).T

        gin_b_ref[...] = stand(gin_b_in[...])[:, 0:1]
        gout_b_ref[...] = dot(turn, stand(gout_b_in[...]).astype(jnp.bfloat16))[:, 0:1]

    @pl.when(step < count_ref[0])
    def _():
        column = column_ref[step]
        base = base_ref[step]
        feat = feat_ref[...]
        vec_t = dot(tower_ref[...], feat, NT).astype(jnp.bfloat16)
        vec_cat = jnp.concatenate([vec_t[b * H : (b + 1) * H] for b in range(K)], axis=1)
        packets = [packet_ref[g, column] for g in range(groups)]
        packed = jnp.concatenate(packets, axis=0)
        vectors = packed[:, :H]
        vectors_t = packed.astype(jnp.float32).T[:H].astype(jnp.bfloat16)
        logit_s[...] = dot(vectors, vec_cat)
        numbers = jnp.concatenate(
            [part.astype(jnp.float32)[:users, H : H + 2 * picks] for part in packets], axis=0
        )
        pos = (numbers[:, :picks] * 128.0 + numbers[:, picks:]).astype(jnp.int32)
        place = base + lax.broadcasted_iota(jnp.int32, (column_users, BLK), 1)
        hit = pos[:, 0:1] == place
        for k in range(1, pos.shape[1]):
            hit = jnp.logical_or(hit, pos[:, k : k + 1] == place)
        target = jnp.where(hit, 1.0, 0.0)
        for first in range(0, column_users, CHUNK):
            picked = range(first, first + CHUNK)
            logits = jnp.concatenate(
                [
                    jnp.concatenate(
                        [
                            logit_s[u * K : (u + 1) * K, b * BLK : (b + 1) * BLK]
                            for b in range(K)
                        ],
                        axis=0,
                    )
                    for u in picked
                ],
                axis=1,
            )
            wanted = jnp.concatenate([target[u : u + 1] for u in picked], axis=1)
            pre = dot(gin_t_ref[...], logits.astype(jnp.bfloat16)) + gin_b_ref[...]
            sig = sigmoid(pre)
            silu = pre * sig
            slope = sig + silu * (1.0 - sig)
            gate = dot(gout_t_ref[...], silu.astype(jnp.bfloat16)) + gout_b_ref[...]
            terms = jnp.exp(gate)
            mixture = terms * (1.0 / jnp.sum(terms, axis=0, keepdims=True))
            scores = jnp.sum(mixture * logits, axis=0, keepdims=True)
            score_grad = sigmoid(scores) - wanted
            weighted = score_grad * mixture
            logit_grad = (weighted * (logits - scores)).astype(jnp.bfloat16)
            hidden_grad = (dot(gout_ref[...], logit_grad) * slope).astype(jnp.bfloat16)
            pair = weighted + dot(gin_ref[...], hidden_grad)
            for n, u in enumerate(picked):
                for b in range(K):
                    pair_s[u * K : (u + 1) * K, b * BLK : (b + 1) * BLK] = pair[
                        b * K : (b + 1) * K, n * BLK : (n + 1) * BLK
                    ]
        pair_all = pair_s[...].astype(jnp.bfloat16)
        uacc[column] += dot(pair_all, vec_cat, NT)
        grad = dot(vectors_t, pair_all).astype(jnp.bfloat16)
        grad_t = jnp.concatenate([grad[:, b * BLK : (b + 1) * BLK] for b in range(K)], axis=0)
        acc[...] += dot(grad_t, feat)

    @pl.when(step == pl.num_programs(0) - 1)
    def _():
        width = acc.shape[1] // owners
        height = acc.shape[0] // groups
        share = rows // groups
        out_ref[...] = jnp.zeros_like(out_ref)
        for g in range(groups):
            for s in range(owners):
                out_ref[g, s, 0:height, 0:width] = acc[
                    g * height : (g + 1) * height, s * width : (s + 1) * width
                ].astype(jnp.bfloat16)
                out_ref[g, s, height : height + share, 0:H] = (
                    uacc[s, g * share : (g + 1) * share] * (1.0 / math.sqrt(H))
                ).astype(jnp.bfloat16)


def sum_kernel(
    groups,
    owners,
    in_ref,
    tower_out,
    user_out,
    recv1,
    stage,
    recv2,
    part,
    final,
    send1,
    rsem1,
    send2,
    rsem2,
    send3,
    rsem3,
):
    g = lax.axis_index("blk")
    s = lax.axis_index("shard")
    height = part.shape[0]
    width = tower_out.shape[0]

    barrier = pltpu.get_barrier_semaphore()
    for d in range(1, groups):
        pl.semaphore_signal(
            barrier, inc=1, device_id=(lax.rem(g + d, groups), s),
            device_id_type=pl.DeviceIdType.MESH,
        )
    for d in range(1, owners):
        pl.semaphore_signal(
            barrier, inc=1, device_id=(g, lax.rem(s + d, owners)),
            device_id_type=pl.DeviceIdType.MESH,
        )
    pl.semaphore_wait(barrier, groups + owners - 2)

    copies = []
    for d in range(1, groups):
        to = lax.rem(g + d, groups)
        copy = pltpu.make_async_remote_copy(
            src_ref=in_ref.at[to], dst_ref=recv1.at[d - 1],
            send_sem=send1.at[d - 1], recv_sem=rsem1.at[d - 1],
            device_id=(to, s), device_id_type=pl.DeviceIdType.MESH,
        )
        copy.start()
        copies.append(copy)
    for copy in copies:
        copy.wait()
    total = in_ref[g].astype(jnp.float32)
    for d in range(1, groups):
        total = total + recv1[d - 1].astype(jnp.float32)
    stage[...] = total.astype(jnp.bfloat16)

    copies = []
    for d in range(1, owners):
        to = lax.rem(s + d, owners)
        copy = pltpu.make_async_remote_copy(
            src_ref=stage.at[to], dst_ref=recv2.at[d - 1],
            send_sem=send2.at[d - 1], recv_sem=rsem2.at[d - 1],
            device_id=(g, to), device_id_type=pl.DeviceIdType.MESH,
        )
        copy.start()
        copies.append(copy)
    for copy in copies:
        copy.wait()
    mine = stage[s].astype(jnp.float32)
    for d in range(1, owners):
        mine = mine + recv2[d - 1].astype(jnp.float32)
    user_out[...] = mine[height:, :]
    part[...] = mine[:height, :]

    copies = []
    for d in range(1, groups):
        to = lax.rem(g + d, groups)
        copy = pltpu.make_async_remote_copy(
            src_ref=part, dst_ref=final.at[g],
            send_sem=send3.at[d - 1], recv_sem=rsem3.at[d - 1],
            device_id=(to, s), device_id_type=pl.DeviceIdType.MESH,
        )
        copy.start()
        copies.append(copy)
    final[g] = part[...]
    for copy in copies:
        copy.wait()
    for r in range(groups):
        tower_out[:, r * height : (r + 1) * height] = final[r].T[:width]


def gather_kernel(groups, owners, in_ref, out_ref, held, own_sem, send1, rsem1, send2, rsem2):
    g = lax.axis_index("blk")
    s = lax.axis_index("shard")
    barrier = pltpu.get_barrier_semaphore()
    for d in range(1, groups):
        pl.semaphore_signal(
            barrier, inc=1, device_id=(lax.rem(g + d, groups), s),
            device_id_type=pl.DeviceIdType.MESH,
        )
    for d in range(1, owners):
        pl.semaphore_signal(
            barrier, inc=1, device_id=(g, lax.rem(s + d, owners)),
            device_id_type=pl.DeviceIdType.MESH,
        )
    pl.semaphore_wait(barrier, groups + owners - 2)

    copies = []
    for d in range(1, owners):
        copy = pltpu.make_async_remote_copy(
            src_ref=in_ref, dst_ref=held.at[g, s],
            send_sem=send1.at[d - 1], recv_sem=rsem1.at[d - 1],
            device_id=(g, lax.rem(s + d, owners)), device_id_type=pl.DeviceIdType.MESH,
        )
        copy.start()
        copies.append(copy)
    own = pltpu.make_async_copy(in_ref, held.at[g, s], own_sem)
    own.start()
    own.wait()
    for copy in copies:
        copy.wait()

    copies = []
    for d in range(1, groups):
        copy = pltpu.make_async_remote_copy(
            src_ref=held.at[g], dst_ref=held.at[g],
            send_sem=send2.at[d - 1], recv_sem=rsem2.at[d - 1],
            device_id=(lax.rem(g + d, groups), s), device_id_type=pl.DeviceIdType.MESH,
        )
        copy.start()
        copies.append(copy)
    for copy in copies:
        copy.wait()
    out_ref[...] = held[...]


def shards(
    item_features,
    tower_weight,
    gate_in,
    gate_in_bias,
    gate_out,
    gate_out_bias,
    user_table,
    user_ids,
    positive_item,
    listed_owner,
    listed_slot,
):
    groups = lax.axis_size("blk")
    owners = lax.axis_size("shard")
    g = lax.axis_index("blk")
    s = lax.axis_index("shard")
    trainers = groups * owners
    listings = listed_slot.shape[0]
    users, picks = positive_item.shape
    table = user_table.shape[0]
    features = item_features.shape[1]
    embed = tower_weight.shape[1]
    hidden = gate_in.shape[1]
    column_users = groups * users
    rows = column_users * K
    circle_part = listings * BLK

    row_match = user_ids[:, None] == jnp.arange(table, dtype=jnp.int32)[None, :]
    user_rows = jnp.dot(
        row_match.astype(jnp.bfloat16), user_table, preferred_element_type=jnp.float32
    ).astype(jnp.bfloat16)
    vectors = (user_rows.astype(jnp.float32) * (1.0 / math.sqrt(H))).astype(jnp.bfloat16)
    vectors = vectors.reshape(users * K, H)
    digits = jnp.concatenate([positive_item // 128, positive_item % 128], axis=1)
    lines = jnp.zeros((users * K, H), jnp.int32)
    lines = lax.dynamic_update_slice(lines, digits, (0, 0))
    lines = lax.dynamic_update_slice(lines, listed_owner.T, (users, 0))
    lines = lax.dynamic_update_slice(lines, listed_slot[None, :], (users + 1, 0))
    packet = jnp.concatenate([vectors, lines.astype(jnp.bfloat16)], axis=1)
    gathered = pl.pallas_call(
        functools.partial(gather_kernel, groups, owners),
        out_shape=jax.ShapeDtypeStruct((groups, owners, users * K, 2 * H), jnp.bfloat16),
        in_specs=[pl.BlockSpec(memory_space=pltpu.VMEM)],
        out_specs=pl.BlockSpec(memory_space=pltpu.VMEM),
        scratch_shapes=[
            pltpu.VMEM((groups, owners, users * K, 2 * H), jnp.bfloat16),
            pltpu.SemaphoreType.DMA,
            pltpu.SemaphoreType.DMA((owners - 1,)),
            pltpu.SemaphoreType.DMA((owners - 1,)),
            pltpu.SemaphoreType.DMA((groups - 1,)),
            pltpu.SemaphoreType.DMA((groups - 1,)),
        ],
        compiler_params=pltpu.CompilerParams(collective_id=1, has_side_effects=True),
    )(packet)
    asked = gathered[:, :, users : users + 2, H : H + listings].astype(jnp.float32)
    asked = asked.astype(jnp.int32)
    all_owner = asked[:, :, 0].reshape(-1)
    all_slot = asked[:, :, 1].reshape(-1)

    entries = trainers * listings
    most = -(-trainers * min(CAP, listings) // groups)
    entry = jnp.arange(entries, dtype=jnp.int32)
    own = all_owner == s
    rank = jnp.sum(
        jnp.where(jnp.logical_and(own[None, :], entry[None, :] < entry[:, None]), 1, 0), axis=1
    )
    count = (jnp.sum(own.astype(jnp.int32)) - g + groups - 1) // groups
    place = jnp.minimum(jnp.arange(most, dtype=jnp.int32), jnp.maximum(count - 1, 0))
    chosen = jnp.logical_and(own[None, :], rank[None, :] == place[:, None] * groups + g)

    def choose(values):
        return jnp.sum(jnp.where(chosen, values[None, :], 0), axis=1)

    trainer = entry // listings
    unit_block = choose(all_slot)
    unit_column = choose(trainer % owners)
    unit_base = choose((trainer // owners) * circle_part + (entry % listings) * BLK)

    height = embed // groups
    width = features // owners
    out_rows = height + users * K

    def whole(shape):
        return pl.BlockSpec(shape, lambda i, *_: (0,) * len(shape))

    terms = pl.pallas_call(
        functools.partial(pair_kernel, groups, owners, users, picks=picks),
        grid_spec=pltpu.PrefetchScalarGridSpec(
            num_scalar_prefetch=4,
            grid=(most,),
            in_specs=[
                pl.BlockSpec((BLK, features), lambda i, c, b, *_: (b[i], 0)),
                whole((embed, features)),
                whole((groups, owners, users * K, 2 * H)),
                whole((K * K, hidden)),
                whole((1, hidden)),
                whole((hidden, K * K)),
                whole((1, K * K)),
            ],
            out_specs=whole((groups, owners, out_rows, LANES)),
            scratch_shapes=[
                pltpu.VMEM((embed, features), jnp.float32),
                pltpu.VMEM((owners, rows, H), jnp.float32),
                pltpu.VMEM((rows, K * BLK), jnp.float32),
                pltpu.VMEM((rows, K * BLK), jnp.float32),
                pltpu.VMEM((K * K, hidden), jnp.bfloat16),
                pltpu.VMEM((hidden, K * K), jnp.bfloat16),
                pltpu.VMEM((hidden, 1), jnp.float32),
                pltpu.VMEM((hidden, K * K), jnp.bfloat16),
                pltpu.VMEM((K * K, hidden), jnp.bfloat16),
                pltpu.VMEM((K * K, 1), jnp.float32),
            ],
        ),
        out_shape=jax.ShapeDtypeStruct((groups, owners, out_rows, LANES), jnp.bfloat16),
        compiler_params=pltpu.CompilerParams(
            dimension_semantics=("arbitrary",), vmem_limit_bytes=56 << 20
        ),
    )(
        count.reshape(1),
        unit_block,
        unit_column,
        unit_base,
        item_features,
        tower_weight.T,
        gathered,
        gate_in,
        gate_in_bias[None, :],
        gate_out,
        gate_out_bias[None, :],
    )

    tower_gradient, user_terms = pl.pallas_call(
        functools.partial(sum_kernel, groups, owners),
        out_shape=(
            jax.ShapeDtypeStruct((width, embed), jnp.float32),
            jax.ShapeDtypeStruct((users * K, LANES), jnp.float32),
        ),
        in_specs=[pl.BlockSpec(memory_space=pltpu.VMEM)],
        out_specs=(
            pl.BlockSpec(memory_space=pltpu.VMEM),
            pl.BlockSpec(memory_space=pltpu.VMEM),
        ),
        scratch_shapes=[
            pltpu.VMEM((groups - 1, owners, out_rows, LANES), jnp.bfloat16),
            pltpu.VMEM((owners, out_rows, LANES), jnp.bfloat16),
            pltpu.VMEM((owners - 1, out_rows, LANES), jnp.bfloat16),
            pltpu.VMEM((height, LANES), jnp.float32),
            pltpu.VMEM((groups, height, LANES), jnp.float32),
            pltpu.SemaphoreType.DMA((groups - 1,)),
            pltpu.SemaphoreType.DMA((groups - 1,)),
            pltpu.SemaphoreType.DMA((owners - 1,)),
            pltpu.SemaphoreType.DMA((owners - 1,)),
            pltpu.SemaphoreType.DMA((groups - 1,)),
            pltpu.SemaphoreType.DMA((groups - 1,)),
        ],
        compiler_params=pltpu.CompilerParams(collective_id=0, has_side_effects=True),
    )(terms)

    user_delta = user_terms[:, :H].reshape(users, embed)
    user_gradient = jnp.sum(
        jnp.where(row_match[:, :, None], user_delta[:, None, :], 0.0), axis=0
    )
    return (tower_gradient, user_gradient)


def solution(mesh):
    return jax.shard_map(
        shards,
        mesh=mesh,
        in_specs=(
            P("shard", None),
            P(),
            P(),
            P(),
            P(),
            P(),
            P(("blk", "shard"), None),
            P(("blk", "shard")),
            P(("blk", "shard"), None),
            P(("blk", "shard"), None),
            P(("blk", "shard")),
        ),
        out_specs=(P("shard", None), P(("blk", "shard"), None)),
        check_vma=False,
    )
```

```python
import functools
import math

import jax
import jax.numpy as jnp
from jax import lax
from jax.experimental import pallas as pl
from jax.experimental.pallas import tpu as pltpu
from jax.sharding import PartitionSpec as P

K = 8
H = 64
BLK = 128
CAP = 2
LANES = 128
CHUNK = 16
CORES = 2

NN = (((1,), (0,)), ((), ()))
NT = (((1,), (1,)), ((), ()))


def dot(left, right, dims=NN):
    return lax.dot_general(left, right, dims, preferred_element_type=jnp.float32)


def sigmoid(v):
    return 0.5 + 0.5 * jnp.tanh(0.5 * v)


def pair_kernel(
    groups,
    owners,
    users,
    count_ref,
    block_ref,
    column_ref,
    base_ref,
    feat_ref,
    tower_ref,
    packet_ref,
    gin_in,
    gin_b_in,
    gout_in,
    gout_b_in,
    out_ref,
    acc,
    uacc,
    logit_s,
    pair_s,
    gin_ref,
    gin_t_ref,
    gin_b_ref,
    gout_ref,
    gout_t_ref,
    gout_b_ref,
    *,
    picks,
):
    step = pl.program_id(0)
    column_users = groups * users
    rows = column_users * K

    @pl.when(step == 0)
    def _():
        acc[...] = jnp.zeros_like(acc)
        uacc[...] = jnp.zeros_like(uacc)
        pairs = K * K
        to = lax.broadcasted_iota(jnp.int32, (pairs, pairs), 0)
        of = lax.broadcasted_iota(jnp.int32, (pairs, pairs), 1)
        turn = jnp.where(of == (to % K) * K + to // K, 1.0, 0.0).astype(jnp.bfloat16)
        gin = dot(turn, gin_in[...])
        gin_ref[...] = gin.astype(jnp.bfloat16)
        gin_t_ref[...] = gin.T.astype(jnp.bfloat16)
        gout_t = dot(turn, gout_in[...])
        gout_t_ref[...] = gout_t.astype(jnp.bfloat16)
        gout_ref[...] = gout_t.T.astype(jnp.bfloat16)

        def stand(row):
            return jnp.broadcast_to(row.astype(jnp.float32), (LANES, row.shape[1])).T

        gin_b_ref[...] = stand(gin_b_in[...])[:, 0:1]
        gout_b_ref[...] = dot(turn, stand(gout_b_in[...]).astype(jnp.bfloat16))[:, 0:1]

    @pl.when(step < count_ref[0])
    def _():
        column = column_ref[step]
        base = base_ref[step]
        feat = feat_ref[...]
        vec_t = dot(tower_ref[...], feat, NT).astype(jnp.bfloat16)
        vec_cat = jnp.concatenate([vec_t[b * H : (b + 1) * H] for b in range(K)], axis=1)
        packets = [packet_ref[g, column] for g in range(groups)]
        packed = jnp.concatenate(packets, axis=0)
        vectors = packed[:, :H]
        vectors_t = packed.astype(jnp.float32).T[:H].astype(jnp.bfloat16)
        logit_s[...] = dot(vectors, vec_cat)
        numbers = jnp.concatenate(
            [part.astype(jnp.float32)[:users, H : H + 2 * picks] for part in packets], axis=0
        )
        pos = (numbers[:, :picks] * 128.0 + numbers[:, picks:]).astype(jnp.int32)
        place = base + lax.broadcasted_iota(jnp.int32, (column_users, BLK), 1)
        hit = pos[:, 0:1] == place
        for k in range(1, pos.shape[1]):
            hit = jnp.logical_or(hit, pos[:, k : k + 1] == place)
        target = jnp.where(hit, 1.0, 0.0)
        for first in range(0, column_users, CHUNK):
            picked = range(first, first + CHUNK)
            logits = jnp.concatenate(
                [
                    jnp.concatenate(
                        [
                            logit_s[u * K : (u + 1) * K, b * BLK : (b + 1) * BLK]
                            for b in range(K)
                        ],
                        axis=0,
                    )
                    for u in picked
                ],
                axis=1,
            )
            wanted = jnp.concatenate([target[u : u + 1] for u in picked], axis=1)
            pre = dot(gin_t_ref[...], logits.astype(jnp.bfloat16)) + gin_b_ref[...]
            sig = sigmoid(pre)
            silu = pre * sig
            slope = sig + silu * (1.0 - sig)
            gate = dot(gout_t_ref[...], silu.astype(jnp.bfloat16)) + gout_b_ref[...]
            terms = jnp.exp(gate)
            mixture = terms * (1.0 / jnp.sum(terms, axis=0, keepdims=True))
            scores = jnp.sum(mixture * logits, axis=0, keepdims=True)
            score_grad = sigmoid(scores) - wanted
            weighted = score_grad * mixture
            logit_grad = (weighted * (logits - scores)).astype(jnp.bfloat16)
            hidden_grad = (dot(gout_ref[...], logit_grad) * slope).astype(jnp.bfloat16)
            pair = weighted + dot(gin_ref[...], hidden_grad)
            for n, u in enumerate(picked):
                for b in range(K):
                    pair_s[u * K : (u + 1) * K, b * BLK : (b + 1) * BLK] = pair[
                        b * K : (b + 1) * K, n * BLK : (n + 1) * BLK
                    ]
        pair_all = pair_s[...].astype(jnp.bfloat16)
        uacc[column] += dot(pair_all, vec_cat, NT)
        grad = dot(vectors_t, pair_all).astype(jnp.bfloat16)
        grad_t = jnp.concatenate([grad[:, b * BLK : (b + 1) * BLK] for b in range(K)], axis=0)
        acc[...] += dot(grad_t, feat)

    @pl.when(step == pl.num_programs(0) - 1)
    def _():
        width = acc.shape[1] // owners
        height = acc.shape[0] // groups
        share = rows // groups
        out_ref[...] = jnp.zeros_like(out_ref)
        for g in range(groups):
            for s in range(owners):
                out_ref[g, s, 0:height, 0:width] = acc[
                    g * height : (g + 1) * height, s * width : (s + 1) * width
                ].astype(jnp.bfloat16)
                out_ref[g, s, height : height + share, 0:H] = (
                    uacc[s, g * share : (g + 1) * share] * (1.0 / math.sqrt(H))
                ).astype(jnp.bfloat16)


def sum_kernel(
    groups,
    owners,
    in_ref,
    tower_out,
    user_out,
    recv0,
    both,
    recv1,
    stage,
    recv2,
    part,
    final,
    send0,
    rsem0,
    send1,
    rsem1,
    send2,
    rsem2,
    send3,
    rsem3,
):
    g = lax.axis_index("blk")
    s = lax.axis_index("shard")
    height = part.shape[0]
    width = tower_out.shape[0]

    barrier = pltpu.get_barrier_semaphore()
    for d in range(1, groups):
        pl.semaphore_signal(
            barrier, inc=1, device_id=(lax.rem(g + d, groups), s),
            device_id_type=pl.DeviceIdType.MESH,
        )
    for d in range(1, owners):
        pl.semaphore_signal(
            barrier, inc=1, device_id=(g, lax.rem(s + d, owners)),
            device_id_type=pl.DeviceIdType.MESH,
        )
    pl.semaphore_wait(barrier, groups + owners - 2)

    half = groups // CORES
    core = lax.rem(g, CORES)
    chip = g // CORES
    other = chip * CORES + (CORES - 1) - core
    first = []
    for d in range(1, half + 1):
        at = lax.rem(chip + d, half)
        copy = pltpu.make_async_remote_copy(
            src_ref=in_ref.at[at * CORES + (CORES - 1) - core], dst_ref=recv0.at[d - 1],
            send_sem=send0.at[d - 1], recv_sem=rsem0.at[d - 1],
            device_id=(other, s), device_id_type=pl.DeviceIdType.MESH,
        )
        copy.start()
        first.append(copy)
    copies = []
    for d in range(1, half):
        to = lax.rem(chip + d, half) * CORES + core
        first[d - 1].wait()
        both[d - 1] = (
            in_ref[to].astype(jnp.float32) + recv0[d - 1].astype(jnp.float32)
        ).astype(jnp.bfloat16)
        copy = pltpu.make_async_remote_copy(
            src_ref=both.at[d - 1], dst_ref=recv1.at[d - 1],
            send_sem=send1.at[d - 1], recv_sem=rsem1.at[d - 1],
            device_id=(to, s), device_id_type=pl.DeviceIdType.MESH,
        )
        copy.start()
        copies.append(copy)
    first[half - 1].wait()
    for copy in copies:
        copy.wait()
    total = in_ref[g].astype(jnp.float32) + recv0[half - 1].astype(jnp.float32)
    for d in range(1, half):
        total = total + recv1[d - 1].astype(jnp.float32)
    stage[...] = total.astype(jnp.bfloat16)

    copies = []
    for d in range(1, owners):
        to = lax.rem(s + d, owners)
        copy = pltpu.make_async_remote_copy(
            src_ref=stage.at[to], dst_ref=recv2.at[d - 1],
            send_sem=send2.at[d - 1], recv_sem=rsem2.at[d - 1],
            device_id=(g, to), device_id_type=pl.DeviceIdType.MESH,
        )
        copy.start()
        copies.append(copy)
    for copy in copies:
        copy.wait()
    mine = stage[s].astype(jnp.float32)
    for d in range(1, owners):
        mine = mine + recv2[d - 1].astype(jnp.float32)
    user_out[...] = mine[height:, :]
    part[...] = mine[:height, :]

    copies = []
    for d in range(1, groups):
        to = lax.rem(g + d, groups)
        copy = pltpu.make_async_remote_copy(
            src_ref=part, dst_ref=final.at[g],
            send_sem=send3.at[d - 1], recv_sem=rsem3.at[d - 1],
            device_id=(to, s), device_id_type=pl.DeviceIdType.MESH,
        )
        copy.start()
        copies.append(copy)
    final[g] = part[...]
    for copy in copies:
        copy.wait()
    for r in range(groups):
        tower_out[:, r * height : (r + 1) * height] = final[r].T[:width]


def gather_kernel(
    groups, owners, in_ref, tower_ref, out_ref, tower_t_ref, held, own_sem, send1, rsem1, send2, rsem2
):
    g = lax.axis_index("blk")
    s = lax.axis_index("shard")
    barrier = pltpu.get_barrier_semaphore()
    for d in range(1, groups):
        pl.semaphore_signal(
            barrier, inc=1, device_id=(lax.rem(g + d, groups), s),
            device_id_type=pl.DeviceIdType.MESH,
        )
    for d in range(1, owners):
        pl.semaphore_signal(
            barrier, inc=1, device_id=(g, lax.rem(s + d, owners)),
            device_id_type=pl.DeviceIdType.MESH,
        )
    pl.semaphore_wait(barrier, groups + owners - 2)

    copies = []
    for d in range(1, owners):
        copy = pltpu.make_async_remote_copy(
            src_ref=in_ref, dst_ref=held.at[g, s],
            send_sem=send1.at[d - 1], recv_sem=rsem1.at[d - 1],
            device_id=(g, lax.rem(s + d, owners)), device_id_type=pl.DeviceIdType.MESH,
        )
        copy.start()
        copies.append(copy)
    own = pltpu.make_async_copy(in_ref, held.at[g, s], own_sem)
    own.start()
    tower_t_ref[...] = tower_ref[...].T
    own.wait()
    for copy in copies:
        copy.wait()

    copies = []
    for d in range(1, groups):
        copy = pltpu.make_async_remote_copy(
            src_ref=held.at[g], dst_ref=held.at[g],
            send_sem=send2.at[d - 1], recv_sem=rsem2.at[d - 1],
            device_id=(lax.rem(g + d, groups), s), device_id_type=pl.DeviceIdType.MESH,
        )
        copy.start()
        copies.append(copy)
    for copy in copies:
        copy.wait()
    out_ref[...] = held[...]


def shards(
    item_features,
    tower_weight,
    gate_in,
    gate_in_bias,
    gate_out,
    gate_out_bias,
    user_table,
    user_ids,
    positive_item,
    listed_owner,
    listed_slot,
):
    groups = lax.axis_size("blk")
    owners = lax.axis_size("shard")
    g = lax.axis_index("blk")
    s = lax.axis_index("shard")
    trainers = groups * owners
    listings = listed_slot.shape[0]
    users, picks = positive_item.shape
    table = user_table.shape[0]
    features = item_features.shape[1]
    embed = tower_weight.shape[1]
    hidden = gate_in.shape[1]
    column_users = groups * users
    rows = column_users * K
    circle_part = listings * BLK

    row_match = user_ids[:, None] == jnp.arange(table, dtype=jnp.int32)[None, :]
    user_rows = jnp.dot(
        row_match.astype(jnp.bfloat16), user_table, preferred_element_type=jnp.float32
    ).astype(jnp.bfloat16)
    vectors = (user_rows.astype(jnp.float32) * (1.0 / math.sqrt(H))).astype(jnp.bfloat16)
    vectors = vectors.reshape(users * K, H)
    digits = jnp.concatenate([positive_item // 128, positive_item % 128], axis=1)
    lines = jnp.zeros((users * K, H), jnp.int32)
    lines = lax.dynamic_update_slice(lines, digits, (0, 0))
    lines = lax.dynamic_update_slice(lines, listed_owner.T, (users, 0))
    lines = lax.dynamic_update_slice(lines, listed_slot[None, :], (users + 1, 0))
    packet = jnp.concatenate([vectors, lines.astype(jnp.bfloat16)], axis=1)
    gathered, tower_t = pl.pallas_call(
        functools.partial(gather_kernel, groups, owners),
        out_shape=(
            jax.ShapeDtypeStruct((groups, owners, users * K, 2 * H), jnp.bfloat16),
            jax.ShapeDtypeStruct((embed, features), jnp.bfloat16),
        ),
        in_specs=[pl.BlockSpec(memory_space=pltpu.VMEM)] * 2,
        out_specs=(pl.BlockSpec(memory_space=pltpu.VMEM),) * 2,
        scratch_shapes=[
            pltpu.VMEM((groups, owners, users * K, 2 * H), jnp.bfloat16),
            pltpu.SemaphoreType.DMA,
            pltpu.SemaphoreType.DMA((owners - 1,)),
            pltpu.SemaphoreType.DMA((owners - 1,)),
            pltpu.SemaphoreType.DMA((groups - 1,)),
            pltpu.SemaphoreType.DMA((groups - 1,)),
        ],
        compiler_params=pltpu.CompilerParams(collective_id=1, has_side_effects=True),
    )(packet, tower_weight)
    asked = gathered[:, :, users : users + 2, H : H + listings].astype(jnp.float32)
    asked = asked.astype(jnp.int32)
    all_owner = asked[:, :, 0].reshape(-1)
    all_slot = asked[:, :, 1].reshape(-1)

    entries = trainers * listings
    most = -(-trainers * min(CAP, listings) // groups)
    entry = jnp.arange(entries, dtype=jnp.int32)
    own = all_owner == s
    rank = jnp.sum(
        jnp.where(jnp.logical_and(own[None, :], entry[None, :] < entry[:, None]), 1, 0), axis=1
    )
    count = (jnp.sum(own.astype(jnp.int32)) - g + groups - 1) // groups
    place = jnp.minimum(jnp.arange(most, dtype=jnp.int32), jnp.maximum(count - 1, 0))
    chosen = jnp.logical_and(own[None, :], rank[None, :] == place[:, None] * groups + g)

    def choose(values):
        return jnp.sum(jnp.where(chosen, values[None, :], 0), axis=1)

    trainer = entry // listings
    unit_block = choose(all_slot)
    unit_column = choose(trainer % owners)
    unit_base = choose((trainer // owners) * circle_part + (entry % listings) * BLK)

    height = embed // groups
    width = features // owners
    out_rows = height + users * K

    def whole(shape):
        return pl.BlockSpec(shape, lambda i, *_: (0,) * len(shape))

    terms = pl.pallas_call(
        functools.partial(pair_kernel, groups, owners, users, picks=picks),
        grid_spec=pltpu.PrefetchScalarGridSpec(
            num_scalar_prefetch=4,
            grid=(most,),
            in_specs=[
                pl.BlockSpec((BLK, features), lambda i, c, b, *_: (b[i], 0)),
                whole((embed, features)),
                whole((groups, owners, users * K, 2 * H)),
                whole((K * K, hidden)),
                whole((1, hidden)),
                whole((K * K, hidden)),
                whole((1, K * K)),
            ],
            out_specs=whole((groups, owners, out_rows, LANES)),
            scratch_shapes=[
                pltpu.VMEM((embed, features), jnp.float32),
                pltpu.VMEM((owners, rows, H), jnp.float32),
                pltpu.VMEM((rows, K * BLK), jnp.float32),
                pltpu.VMEM((rows, K * BLK), jnp.float32),
                pltpu.VMEM((K * K, hidden), jnp.bfloat16),
                pltpu.VMEM((hidden, K * K), jnp.bfloat16),
                pltpu.VMEM((hidden, 1), jnp.float32),
                pltpu.VMEM((hidden, K * K), jnp.bfloat16),
                pltpu.VMEM((K * K, hidden), jnp.bfloat16),
                pltpu.VMEM((K * K, 1), jnp.float32),
            ],
        ),
        out_shape=jax.ShapeDtypeStruct((groups, owners, out_rows, LANES), jnp.bfloat16),
        compiler_params=pltpu.CompilerParams(
            dimension_semantics=("arbitrary",), vmem_limit_bytes=56 << 20
        ),
    )(
        count.reshape(1),
        unit_block,
        unit_column,
        unit_base,
        item_features,
        tower_t,
        gathered,
        gate_in,
        gate_in_bias[None, :],
        gate_out.T,
        gate_out_bias[None, :],
    )

    tower_gradient, user_terms = pl.pallas_call(
        functools.partial(sum_kernel, groups, owners),
        out_shape=(
            jax.ShapeDtypeStruct((width, embed), jnp.float32),
            jax.ShapeDtypeStruct((users * K, LANES), jnp.float32),
        ),
        in_specs=[pl.BlockSpec(memory_space=pltpu.VMEM)],
        out_specs=(
            pl.BlockSpec(memory_space=pltpu.VMEM),
            pl.BlockSpec(memory_space=pltpu.VMEM),
        ),
        scratch_shapes=[
            pltpu.VMEM((groups // CORES, owners, out_rows, LANES), jnp.bfloat16),
            pltpu.VMEM((groups // CORES - 1, owners, out_rows, LANES), jnp.bfloat16),
            pltpu.VMEM((groups // CORES - 1, owners, out_rows, LANES), jnp.bfloat16),
            pltpu.VMEM((owners, out_rows, LANES), jnp.bfloat16),
            pltpu.VMEM((owners - 1, out_rows, LANES), jnp.bfloat16),
            pltpu.VMEM((height, LANES), jnp.float32),
            pltpu.VMEM((groups, height, LANES), jnp.float32),
            pltpu.SemaphoreType.DMA((groups // CORES,)),
            pltpu.SemaphoreType.DMA((groups // CORES,)),
            pltpu.SemaphoreType.DMA((groups // CORES - 1,)),
            pltpu.SemaphoreType.DMA((groups // CORES - 1,)),
            pltpu.SemaphoreType.DMA((owners - 1,)),
            pltpu.SemaphoreType.DMA((owners - 1,)),
            pltpu.SemaphoreType.DMA((groups - 1,)),
            pltpu.SemaphoreType.DMA((groups - 1,)),
        ],
        compiler_params=pltpu.CompilerParams(collective_id=0, has_side_effects=True),
    )(terms)

    user_delta = user_terms[:, :H].reshape(users, embed)
    user_gradient = jnp.sum(
        jnp.where(row_match[:, :, None], user_delta[:, None, :], 0.0), axis=0
    )
    return (tower_gradient, user_gradient)


def solution(mesh):
    return jax.shard_map(
        shards,
        mesh=mesh,
        in_specs=(
            P("shard", None),
            P(),
            P(),
            P(),
            P(),
            P(),
            P(("blk", "shard"), None),
            P(("blk", "shard")),
            P(("blk", "shard"), None),
            P(("blk", "shard"), None),
            P(("blk", "shard")),
        ),
        out_specs=(P("shard", None), P(("blk", "shard"), None)),
        check_vma=False,
    )
```
